32 devices in a mesh: section: 2 (over y), dp: 4 (over x, core), mp: 4 (over z).
Axes of the slice: x: 2, y: 2, z: 4, core: 2. Of those that a mesh axis runs over, the one named last changes fastest.
Arguments:
- activations: bfloat16 [2, 256, 4096], P(None, 'dp'), may hold values from -6 to 6
- cotangent: bfloat16 [2, 256, 4096], P(None, 'dp'), may hold values from -6 to 6
- norm_gain: float32 [2, 4096], P('section'), may hold values from 0.1 to 1.9
- w_up: bfloat16 [2, 4096, 8192], P('section', 'dp', 'mp'), may hold values from -0.09375 to 0.09375
- w_down: bfloat16 [2, 4096, 8192], P('section', 'dp', 'mp'), may hold values from -0.0625 to 0.0625
- gram_left: float32 [2, 128, 512, 512], P('section', ('dp', 'mp')), as said below
- gram_right: float32 [2, 128, 512, 512], P('section', ('dp', 'mp')), as said below
- root_left: bfloat16 [2, 128, 512, 512], P('section', ('dp', 'mp'))
- root_right: bfloat16 [2, 128, 512, 512], P('section', ('dp', 'mp'))
- owner_slot: int32 [2, 16, 8], replicated, may hold values from 0 to 127, as said below
- eighth: int32 [2, 16, 8], replicated, may hold values from 0 to 7, as said below
- refresh_phase: int32 [1], replicated, may hold values from 0 to 999999
Outputs:
- new_gram_left: float32 [2, 128, 512, 512], P('section', ('dp', 'mp'))
- new_gram_right: float32 [2, 128, 512, 512], P('section', ('dp', 'mp'))
- new_root_left: bfloat16 [2, 128, 512, 512], P('section', ('dp', 'mp'))
- new_root_right: bfloat16 [2, 128, 512, 512], P('section', ('dp', 'mp'))
- update_blocks: bfloat16 [2, 128, 512, 512], P('section', ('dp', 'mp'))
The draws below stay inside these ranges and needn't reach their ends.
Inputs may be any that keep to these rules, and one draw needn't show every extreme that they name: `owner_slot`: for each section, a permutation of the 128 slots; the block of flat index f = i * 8 + j goes to a slot t with (t // 8) % (4) == f // 32. `eighth`: in each section and each run of 32 consecutive flat block indices, every value is taken by exactly 4 blocks. `gram_left`: symmetric positive definite. `gram_right`: symmetric positive definite.
All inputs are finite; a program needn't handle non-finite values.
Results may differ from the reference program's by a relative error of at most 0.025.
Values may be sent and summed in bfloat16 or wider, within the bound.
A program may use at most 192 MiB of HBM per device.

```python
import math
import jax
import jax.numpy as jnp
from jax import lax

D = 4096
FFW = 8192
BLK = 512
MB = 2
TOK_MB = 64
ITERS = 2
TOKENS_MB = 256
NROW = 16
NCOL = 8
SLOTS = 128
GROUP = 32
BPD = 8
N_SECTION = 2
N_DP = 4
N_MP = 4


def gram_draw(key, salt):
    inner_key = jax.random.fold_in(key, salt)
    draw_keys = jax.random.split(inner_key, 8)
    top_count = 3
    support_width = max(BLK // 32, 4)
    batch_count = N_SECTION * SLOTS * top_count
    support_keys = jax.random.split(draw_keys[0], batch_count)
    support = jax.vmap(lambda one_key: jax.random.permutation(one_key, BLK)[:support_width])(support_keys)
    onehot = (support[:, :, None] == jnp.arange(BLK, dtype=jnp.int32)[None, None, :]).astype(jnp.float32)
    sign_values = jnp.where(jax.random.bernoulli(draw_keys[1], 0.5, (batch_count, support_width)), 1.0, -1.0).astype(jnp.float32)
    magnitudes = jax.random.uniform(draw_keys[2], (batch_count, support_width), jnp.float32, 0.5, 1.5)
    ratios = jax.random.uniform(draw_keys[3], (N_SECTION, SLOTS, top_count - 1), jnp.float32, 0.3, 0.6)
    top_level = 40.0 * jax.random.uniform(draw_keys[4], (N_SECTION, SLOTS, 1), jnp.float32, 0.8, 1.2)
    factor = jax.random.uniform(draw_keys[5], (N_SECTION, SLOTS, BLK, BLK), jnp.float32, -1.0, 1.0) * math.sqrt(3.0)
    tail_decay = jnp.power(10.0, -3.0 * jax.random.uniform(draw_keys[6], (N_SECTION, SLOTS, BLK), jnp.float32))
    diagonal = jax.random.uniform(draw_keys[7], (N_SECTION, SLOTS, BLK), jnp.float32, 0.05, 0.2)
    entries = sign_values * magnitudes
    vectors = jnp.einsum('bw,bwn->bn', entries, onehot)
    vectors = vectors / jnp.sqrt(jnp.sum(vectors * vectors, axis=-1, keepdims=True))
    vectors = vectors.reshape(N_SECTION, SLOTS, top_count, BLK)
    strengths = top_level * jnp.concatenate([jnp.ones((N_SECTION, SLOTS, 1), jnp.float32), ratios], axis=-1)
    top_part = jnp.einsum('sbk,sbki,sbkj->sbij', strengths, vectors, vectors)
    tail_part = jnp.einsum('sbij,sbj,sbkj->sbik', factor, tail_decay, factor) / BLK
    matrix = top_part + tail_part + diagonal[..., None] * jnp.eye(BLK, dtype=jnp.float32)
    return 0.5 * (matrix + jnp.swapaxes(matrix, -1, -2))


def root_draw(key, salt):
    inner_key = jax.random.fold_in(key, salt)
    key_diag, key_noise = jax.random.split(inner_key, 2)
    diagonal = jax.random.uniform(key_diag, (N_SECTION, SLOTS, BLK), jnp.float32, 0.3, 0.8)
    noise_part = 0.01 * jax.random.normal(key_noise, (N_SECTION, SLOTS, BLK, BLK), jnp.float32)
    matrix = noise_part + diagonal[..., None] * jnp.eye(BLK, dtype=jnp.float32)
    return matrix.astype(jnp.bfloat16)


def group_shuffles(key, salt):
    group_keys = jax.random.split(jax.random.fold_in(key, salt), N_SECTION * N_MP)
    shuffles = jax.vmap(lambda one_key: jax.random.permutation(one_key, GROUP))(group_keys)
    return shuffles.reshape(N_SECTION, N_MP, GROUP).astype(jnp.int32)


def draw_gram_left(key, part):
    return gram_draw(key, 11)


def draw_gram_right(key, part):
    return gram_draw(key, 12)


def draw_root_left(key, part):
    return root_draw(key, 13)


def draw_root_right(key, part):
    return root_draw(key, 14)


def draw_owner_slot(key, part):
    shuffles = group_shuffles(key, 21)
    group_ids = jnp.arange(N_MP, dtype=jnp.int32)[None, :, None]
    slot_values = (shuffles // BPD * N_MP + group_ids) * BPD + shuffles % BPD
    return slot_values.reshape(N_SECTION, NROW, NCOL).astype(jnp.int32)


def draw_eighth(key, part):
    shuffles = group_shuffles(key, 22)
    return (shuffles % 8).reshape(N_SECTION, NROW, NCOL).astype(jnp.int32)


def block_levels(rng, extent, pieces, low, largest):
    factor_of, own = 1.0, jax.random.fold_in(rng, 6)
    for axis_at, blocks in pieces:
        steps = jnp.exp(jax.random.uniform(jax.random.fold_in(own, axis_at), (blocks,), jnp.float32, low / len(pieces), largest / len(pieces)))
        factor_of = factor_of * jnp.repeat(steps, extent[axis_at] // blocks).reshape([-1 if axis == axis_at else 1 for axis in range(len(extent))])
    return factor_of


def noise(rng, dims, scale, reach, cuts=(), kind=jnp.bfloat16):
    result = jax.random.normal(rng, dims, jnp.float32) * scale
    if len(cuts) > 0:
        result = block_levels(rng, dims, cuts, -0.22, 0.18) * result
    return jnp.clip(result, min=-reach, max=reach).astype(kind)


def setup_inputs(seed: int = 0) -> dict:
    key_of = jax.random.split(jax.random.key(seed), 13)
    activations = noise(key_of[0], (MB, TOKENS_MB, D), 1.0, 6.0, ((1, 4),))
    cotangent = noise(key_of[1], (MB, TOKENS_MB, D), 1.0, 6.0, ((1, 4),))
    norm_gain = jnp.clip(1.0 + 0.18 * jax.random.normal(key_of[2], (N_SECTION, D), jnp.float32), 0.1, 1.9)
    w_up = noise(key_of[3], (N_SECTION, D, FFW), D ** -0.5, 0.09375, ((0, 2), (1, 4), (2, 4)))
    w_down = noise(key_of[4], (N_SECTION, D, FFW), FFW ** -0.5, 0.0625, ((0, 2), (1, 4), (2, 4)))
    gram_left = draw_gram_left(jax.random.fold_in(key_of[12], 71), 0)
    gram_right = draw_gram_right(jax.random.fold_in(key_of[12], 71), 0)
    root_left = draw_root_left(jax.random.fold_in(key_of[12], 71), 0)
    root_right = draw_root_right(jax.random.fold_in(key_of[12], 71), 0)
    owner_slot = draw_owner_slot(jax.random.fold_in(key_of[12], 71), 0)
    eighth = draw_eighth(jax.random.fold_in(key_of[12], 71), 0)
    refresh_phase = jax.random.randint(key_of[11], (1,), 0, 1000000).astype(jnp.int32)
    return {"activations": activations, "cotangent": cotangent, "norm_gain": norm_gain, "w_up": w_up, "w_down": w_down, "gram_left": gram_left, "gram_right": gram_right, "root_left": root_left, "root_right": root_right, "owner_slot": owner_slot, "eighth": eighth, "refresh_phase": refresh_phase}


norm_epsilon = 1e-05
decay_rate = 0.9
ridge_shift = 0.001
highest = lax.Precision.HIGHEST

def normalize_values(values, gain_row):
    inverse_rms = lax.rsqrt(lax.optimization_barrier(jnp.mean(values * values, axis=-1, keepdims=True)) + norm_epsilon)
    return values * inverse_rms * gain_row

def silu_slope(pre_act):
    sigmoid_values = jax.nn.sigmoid(pre_act)
    return sigmoid_values * (1.0 + pre_act * (1.0 - sigmoid_values))

def inverse_root(matrix):
    matrix_order = matrix.shape[-1]
    identity = jnp.eye(matrix_order, dtype=jnp.float32)
    shifted = matrix + ridge_shift * identity
    factor = 2.5 / jnp.sqrt(jnp.sum(shifted * shifted))
    iterate = jnp.power(factor, 0.25) * identity
    moment = factor * shifted
    for sweep_no in range(ITERS):
        step_mat = 1.25 * identity - 0.25 * moment
        square = jnp.dot(step_mat, step_mat, precision=highest)
        fourth = jnp.dot(square, square, precision=highest)
        moment = jnp.dot(fourth, moment, precision=highest)
        iterate = jnp.dot(iterate, step_mat, precision=highest)
    return iterate

def split_sum(left_rows, right_rows):
    left_parts = jnp.moveaxis(left_rows.reshape(left_rows.shape[0], N_MP, -1), 1, 0)
    right_parts = jnp.moveaxis(right_rows.reshape(right_rows.shape[0], N_MP, -1), 1, 0)

    def add_part(running_total, pair_in):
        product = lax.dot_general(pair_in[0], pair_in[1], (((1,), (1,)), ((), ())), preferred_element_type=jnp.float32)
        rounded = lax.optimization_barrier(product.astype(jnp.bfloat16)).astype(jnp.float32)
        return (running_total + rounded, None)
    zero_sum = jnp.zeros((left_rows.shape[0], right_rows.shape[0]), jnp.float32)
    running_total, unused = lax.scan(add_part, zero_sum, (left_parts, right_parts))
    return running_total

def forward_layer(inputs, gain_row, up_rows, down_rows):
    values = inputs.astype(jnp.float32)
    normed = normalize_values(values, gain_row).astype(jnp.bfloat16)
    pre_act = jnp.dot(normed, up_rows, preferred_element_type=jnp.float32)
    hidden = jax.nn.silu(pre_act).astype(jnp.bfloat16)
    output = (values + split_sum(hidden, down_rows)).astype(jnp.bfloat16)
    return (output, pre_act, hidden)

def backward_layer(grad_output, inputs, pre_act, gain_row, up_rows, down_rows):
    grad_hidden = jnp.dot(grad_output, down_rows, preferred_element_type=jnp.float32)
    grad_pre = (grad_hidden * silu_slope(pre_act)).astype(jnp.bfloat16)
    grad_normed = split_sum(grad_pre, up_rows)
    values = inputs.astype(jnp.float32)
    unused, pullback = jax.vjp(lambda values_in: normalize_values(values_in, gain_row), values)
    grad_values = pullback(grad_normed)[0]
    return (grad_output.astype(jnp.float32) + grad_values).astype(jnp.bfloat16)

def reference(activations, cotangent, norm_gain, w_up, w_down, gram_left, gram_right, root_left, root_right, owner_slot, eighth, refresh_phase):
    section_total = w_up.shape[0]
    micro_count, token_rows, model_width = activations.shape
    flat_rows = micro_count * token_rows
    layer_in = activations.reshape(flat_rows, model_width)
    section_saved = []
    for section_no in range(section_total):
        output, pre_act, hidden = forward_layer(layer_in, norm_gain[section_no], w_up[section_no], w_down[section_no])
        section_saved.append((layer_in, pre_act, hidden))
        layer_in = output
    grad_output = cotangent.reshape(flat_rows, model_width)
    section_grads = [None] * section_total
    for section_no in reversed(range(section_total)):
        inputs, pre_act, hidden = section_saved[section_no]
        section_grads[section_no] = (hidden, grad_output)
        if section_no > 0:
            grad_output = backward_layer(grad_output, inputs, pre_act, norm_gain[section_no], w_up[section_no], w_down[section_no])
    phase_now = refresh_phase[0] % 8
    gram_lefts, gram_rights, root_lefts, root_rights, updates = ([], [], [], [], [])
    for section_no in range(section_total):
        hidden, grad_out = section_grads[section_no]
        hidden_rep = hidden.reshape(micro_count, N_DP, TOK_MB, FFW).transpose(1, 0, 2, 3).reshape(N_DP, micro_count * TOK_MB, FFW)
        grad_rep = grad_out.reshape(micro_count, N_DP, TOK_MB, model_width).transpose(1, 0, 2, 3).reshape(N_DP, micro_count * TOK_MB, model_width)

        def add_replica(running_total, pair_in):
            product = lax.dot_general(pair_in[0], pair_in[1], (((0,), (0,)), ((), ())), preferred_element_type=jnp.float32)
            rounded = lax.optimization_barrier(product.astype(jnp.bfloat16)).astype(jnp.float32)
            return (running_total + rounded, None)
        zero_sum = jnp.zeros((FFW, model_width), jnp.float32)
        summed, unused = lax.scan(add_replica, zero_sum, (hidden_rep, grad_rep))
        scaled = summed * (1.0 / math.sqrt(micro_count * token_rows))
        blocks = scaled.reshape(NROW, BLK, NCOL, BLK).transpose(0, 2, 1, 3).reshape(SLOTS, BLK, BLK)
        block_of_slot = jnp.argsort(owner_slot[section_no].reshape(-1)).astype(jnp.int32)
        slot_grad = blocks[block_of_slot]
        is_due = eighth[section_no].reshape(-1)[block_of_slot] == phase_now
        left_new = decay_rate * gram_left[section_no] + jnp.einsum('sij,skj->sik', slot_grad, slot_grad, precision=highest) / BLK
        right_new = decay_rate * gram_right[section_no] + jnp.einsum('sji,sjk->sik', slot_grad, slot_grad, precision=highest) / BLK
        due_slots = jnp.argsort(jnp.logical_not(is_due).astype(jnp.int32), stable=True)[:SLOTS // 8].astype(jnp.int32)
        fresh_left = jax.vmap(inverse_root)(left_new[due_slots]).astype(jnp.bfloat16)
        fresh_right = jax.vmap(inverse_root)(right_new[due_slots]).astype(jnp.bfloat16)
        roots_l = root_left[section_no].at[due_slots].set(fresh_left)
        roots_r = root_right[section_no].at[due_slots].set(fresh_right)
        grad_low = slot_grad.astype(jnp.bfloat16)
        inner_product = jnp.einsum('sij,sjk->sik', grad_low.astype(jnp.float32), roots_r.astype(jnp.float32), precision=highest).astype(jnp.bfloat16)
        update = jnp.einsum('sij,sjk->sik', roots_l.astype(jnp.float32), inner_product.astype(jnp.float32), precision=highest).astype(jnp.bfloat16)
        gram_lefts.append(left_new)
        gram_rights.append(right_new)
        root_lefts.append(roots_l)
        root_rights.append(roots_r)
        updates.append(update)
    return (jnp.stack(gram_lefts), jnp.stack(gram_rights), jnp.stack(root_lefts), jnp.stack(root_rights), jnp.stack(updates))
```

```python
import math

import jax
import jax.numpy as jnp
from jax import lax
from jax.experimental import pallas as pl
from jax.experimental.pallas import tpu as pltpu
from jax.sharding import PartitionSpec as P

BLK = 512
MESH = pl.DeviceIdType.MESH
VMEM_LIMIT = 60 * 1024 * 1024

norm_epsilon = 1e-05
decay_rate = 0.9
ridge_shift = 0.001


def meet(devices):
    barrier = pltpu.get_barrier_semaphore()
    for device in devices:
        pl.semaphore_signal(barrier, inc=1, device_id=device, device_id_type=MESH)
    pl.semaphore_wait(barrier, len(devices))


def exchange(collective_id, srcs, out_lead, drop_lead, plan):
    count = len(srcs)
    with_keep = plan.keeps
    copy_total = plan.copies * count

    def kernel(*refs):
        ins, outs = refs[:count], refs[count : 2 * count]
        send_sem, recv_sem, keep_sem = refs[2 * count :]
        items, keep = plan()
        meet([device for _, _, device in items])
        copies = []
        for item_no, (src_index, dst_index, device) in enumerate(items):
            for part_no in range(count):
                at = item_no * count + part_no
                copy = pltpu.make_async_remote_copy(
                    src_ref=ins[part_no].at[src_index],
                    dst_ref=outs[part_no].at[dst_index],
                    send_sem=send_sem.at[at],
                    recv_sem=recv_sem.at[at],
                    device_id=device,
                    device_id_type=MESH,
                )
                copy.start()
                copies.append(copy)
        kept = []
        if with_keep:
            for part_no in range(count):
                copy = pltpu.make_async_copy(
                    ins[part_no].at[keep[0]], outs[part_no].at[keep[1]], keep_sem.at[part_no]
                )
                copy.start()
                kept.append(copy)
        for copy in kept + copies:
            copy.wait()

    return pl.pallas_call(
        kernel,
        out_shape=[
            jax.ShapeDtypeStruct(out_lead + src.shape[drop_lead:], src.dtype) for src in srcs
        ],
        in_specs=[pl.BlockSpec(memory_space=pltpu.VMEM)] * count,
        out_specs=[pl.BlockSpec(memory_space=pl.ANY)] * count,
        scratch_shapes=[
            pltpu.SemaphoreType.DMA((copy_total,)),
            pltpu.SemaphoreType.DMA((copy_total,)),
            pltpu.SemaphoreType.DMA((count,)),
        ],
        compiler_params=pltpu.CompilerParams(
            collective_id=collective_id, has_side_effects=True, vmem_limit_bytes=VMEM_LIMIT
        ),
    )(*srcs)


class Plan:
    def __init__(self, copies, keeps, build):
        self.copies, self.keeps, self.build = copies, keeps, build

    def __call__(self):
        return self.build()


def swap_slots(collective_id, srcs, axis):
    size = lax.axis_size(axis)

    def build():
        me = lax.axis_index(axis)
        items = []
        for step in range(1, size):
            other = lax.rem(me + step, size)
            items.append(((other,), (me,), {axis: other}))
        return items, ((me,), (me,))

    return exchange(collective_id, srcs, (size,), 1, Plan(size - 1, True, build))


def scatter_slots(collective_id, srcs, axis, stride=1):
    size = lax.axis_size(axis) // stride

    def build():
        position = lax.axis_index(axis)
        me, rest = position // stride, lax.rem(position, stride)
        items = []
        for step in range(1, size):
            other = lax.rem(me + step, size)
            items.append(((other,), (step - 1,), {axis: other * stride + rest}))
        return items, None

    return exchange(collective_id, srcs, (size - 1,), 1, Plan(size - 1, False, build))


def pair_half(collective_id, srcs):
    chips = lax.axis_size("dp") // 2

    def build():
        me = lax.axis_index("dp")
        core = lax.rem(me, 2)
        other = 1 - core
        return [((slice(None), other), (slice(None),), {"dp": me - core + other})], None

    return exchange(collective_id, srcs, (chips,), 2, Plan(1, False, build))


def gather_across(collective_id, srcs):
    size = lax.axis_size("mp")

    def build():
        me = lax.axis_index("mp")
        far = 1 - lax.axis_index("section")
        items = []
        for step in range(size):
            other = lax.rem(me + step, size)
            items.append(((0,), (me,), {"section": far, "mp": other}))
        return items, None

    return exchange(
        collective_id, [src[None] for src in srcs], (size,), 1, Plan(size, False, build)
    )


def gather_dp(collective_id, srcs):
    count = len(srcs)
    chips = lax.axis_size("dp") // 2

    def kernel(*refs):
        ins, outs = refs[:count], refs[count : 2 * count]
        send_sem, recv_sem, pair_send, pair_recv, keep_sem = refs[2 * count :]
        position = lax.axis_index("dp")
        chip, core = position // 2, lax.rem(position, 2)
        partner = chip * 2 + 1 - core
        others = [lax.rem(chip + step, chips) for step in range(1, chips)]
        meet([{"dp": partner}] + [{"dp": other * 2 + core} for other in others])
        away, handed, kept = [], [], []
        for step, other in enumerate(others):
            for part_no in range(count):
                at = step * count + part_no
                copy = pltpu.make_async_remote_copy(
                    src_ref=ins[part_no],
                    dst_ref=outs[part_no].at[chip, core],
                    send_sem=send_sem.at[at],
                    recv_sem=recv_sem.at[at],
                    device_id={"dp": other * 2 + core},
                    device_id_type=MESH,
                )
                copy.start()
                away.append(copy)
        for part_no in range(count):
            copy = pltpu.make_async_remote_copy(
                src_ref=ins[part_no],
                dst_ref=outs[part_no].at[chip, core],
                send_sem=pair_send.at[part_no],
                recv_sem=pair_recv.at[part_no],
                device_id={"dp": partner},
                device_id_type=MESH,
            )
            copy.start()
            handed.append(copy)
            copy = pltpu.make_async_copy(
                ins[part_no], outs[part_no].at[chip, core], keep_sem.at[part_no]
            )
            copy.start()
            kept.append(copy)
        for step in range(1, chips):
            source = lax.rem(chip + chips - step, chips)
            for part_no in range(count):
                away[(step - 1) * count + part_no].wait_recv()
                at = step * count + part_no
                copy = pltpu.make_async_remote_copy(
                    src_ref=outs[part_no].at[source, core],
                    dst_ref=outs[part_no].at[source, core],
                    send_sem=pair_send.at[at],
                    recv_sem=pair_recv.at[at],
                    device_id={"dp": partner},
                    device_id_type=MESH,
                )
                copy.start()
                handed.append(copy)
        for copy in away:
            copy.wait_send()
        for copy in handed + kept:
            copy.wait()

    return pl.pallas_call(
        kernel,
        out_shape=[jax.ShapeDtypeStruct((chips, 2) + src.shape, src.dtype) for src in srcs],
        in_specs=[pl.BlockSpec(memory_space=pltpu.VMEM)] * count,
        out_specs=[pl.BlockSpec(memory_space=pl.ANY)] * count,
        scratch_shapes=[
            pltpu.SemaphoreType.DMA(((chips - 1) * count,)),
            pltpu.SemaphoreType.DMA(((chips - 1) * count,)),
            pltpu.SemaphoreType.DMA((chips * count,)),
            pltpu.SemaphoreType.DMA((chips * count,)),
            pltpu.SemaphoreType.DMA((count,)),
        ],
        compiler_params=pltpu.CompilerParams(
            collective_id=collective_id, has_side_effects=True, vmem_limit_bytes=VMEM_LIMIT
        ),
    )(*srcs)


def reduce_dp(first_id, product, row_sums):
    total, rows, columns = product.shape
    chips = total // 2
    position = lax.axis_index("dp")
    chip, core = position // 2, position % 2
    parts = [
        product.reshape(chips, 2, rows, columns),
        jnp.broadcast_to(row_sums[:, None, :], (total, 8, rows)).reshape(chips, 2, 8, rows),
    ]
    received = pair_half(first_id, parts)
    halves = [
        (
            lax.dynamic_index_in_dim(part, core, 1, keepdims=False).astype(jnp.float32)
            + other.astype(jnp.float32)
        ).astype(part.dtype)
        for part, other in zip(parts, received)
    ]
    received = scatter_slots(first_id + 1, halves, "dp", 2)
    summed = [
        lax.dynamic_index_in_dim(half, chip, 0, keepdims=False).astype(jnp.float32)
        + jnp.sum(other.astype(jnp.float32), axis=0)
        for half, other in zip(halves, received)
    ]
    return summed[0], summed[1][0]


def reduce_mp(collective_id, srcs):
    me = lax.axis_index("mp")
    received = scatter_slots(collective_id, srcs, "mp")
    return [
        lax.dynamic_index_in_dim(src, me, 0, keepdims=False).astype(jnp.float32)
        + jnp.sum(other.astype(jnp.float32), axis=0)
        for src, other in zip(srcs, received)
    ]


def silu_slope(pre_act):
    sigmoid_values = jax.nn.sigmoid(pre_act)
    return sigmoid_values * (1.0 + pre_act * (1.0 - sigmoid_values))


def matmul(left, right, left_dim=1, right_dim=0):
    return lax.dot_general(
        left, right, (((left_dim,), (right_dim,)), ((), ())), preferred_element_type=jnp.float32
    )


def inverse_root(matrix):
    low = jnp.bfloat16
    order = matrix.shape[-1]
    on_diagonal = lax.broadcasted_iota(jnp.int32, (order, order), 0) == lax.broadcasted_iota(
        jnp.int32, (order, order), 1
    )
    identity = jnp.where(on_diagonal, 1.0, 0.0).astype(jnp.float32)
    shifted = matrix + ridge_shift * identity
    norm_sq = jnp.sum(jnp.sum(shifted * shifted, axis=1, keepdims=True), axis=0, keepdims=True)
    factor = 2.5 / jnp.sqrt(norm_sq)
    moment = factor * shifted
    moment_low = moment.astype(low)
    moment_sq = matmul(moment_low, moment_low)
    square = (1.5625 * identity - 0.625 * moment + 0.0625 * moment_sq).astype(low)
    stepped = (1.25 * moment - 0.25 * moment_sq).astype(low)
    third = matmul(square, stepped).astype(low)
    fifth = matmul(square, third)
    scale = jnp.sqrt(jnp.sqrt(factor))
    return scale * (1.5625 * identity - 0.3125 * moment - 0.25 * fifth)


def precondition(block_row, block_col, due, hidden, grads, gram_l, gram_r, root_l, root_r):
    slots = gram_l.shape[0]
    tokens = hidden.shape[0]
    width = grads.shape[2]
    scale = 1.0 / math.sqrt(tokens)

    def kernel(
        row_ref, col_ref, due_ref, hid_ref, grad_ref, gl_ref, gr_ref, rl_ref, rr_ref,
        gl_out, gr_out, rl_out, rr_out, up_out,
    ):
        slot = pl.program_id(0)
        pieces = [grad_ref[piece] for piece in range(grad_ref.shape[0])]
        dy = pieces[0] if len(pieces) == 1 else jnp.concatenate(pieces, axis=1)
        grad_low = (matmul(hid_ref[...], dy, 0, 0) * scale).astype(jnp.bfloat16)
        gl_out[0] = decay_rate * gl_ref[0] + matmul(grad_low, grad_low, 1, 1) * (1.0 / BLK)
        gr_out[0] = decay_rate * gr_ref[0] + matmul(grad_low, grad_low, 0, 0) * (1.0 / BLK)

        @pl.when(due_ref[slot] != 0)
        def _():
            rl_out[0] = inverse_root(gl_out[0]).astype(jnp.bfloat16)
            rr_out[0] = inverse_root(gr_out[0]).astype(jnp.bfloat16)

        @pl.when(due_ref[slot] == 0)
        def _():
            rl_out[0] = rl_ref[0]
            rr_out[0] = rr_ref[0]

        right_part = matmul(grad_low, rr_out[0]).astype(jnp.bfloat16)
        up_out[0] = matmul(rl_out[0], right_part).astype(jnp.bfloat16)

    if width >= BLK:
        per = width // BLK
        grad_spec = pl.BlockSpec(
            (1, tokens, BLK),
            lambda s, row, col, due: (lax.div(col[s], per), 0, lax.rem(col[s], per)),
        )
    else:
        grad_spec = pl.BlockSpec(
            (BLK // width, tokens, width), lambda s, row, col, due: (col[s], 0, 0)
        )
    square_spec = pl.BlockSpec((1, BLK, BLK), lambda s, row, col, due: (s, 0, 0))
    return pl.pallas_call(
        kernel,
        grid_spec=pltpu.PrefetchScalarGridSpec(
            num_scalar_prefetch=3,
            grid=(slots,),
            in_specs=[
                pl.BlockSpec((tokens, BLK), lambda s, row, col, due: (0, row[s])),
                grad_spec,
            ]
            + [square_spec] * 4,
            out_specs=[square_spec] * 5,
        ),
        out_shape=[
            jax.ShapeDtypeStruct(gram_l.shape, jnp.float32),
            jax.ShapeDtypeStruct(gram_l.shape, jnp.float32),
            jax.ShapeDtypeStruct(gram_l.shape, jnp.bfloat16),
            jax.ShapeDtypeStruct(gram_l.shape, jnp.bfloat16),
            jax.ShapeDtypeStruct(gram_l.shape, jnp.bfloat16),
        ],
        compiler_params=pltpu.CompilerParams(
            dimension_semantics=("arbitrary",), vmem_limit_bytes=VMEM_LIMIT
        ),
    )(block_row, block_col, due, hidden, grads, gram_l, gram_r, root_l, root_r)


def on_device(
    activations,
    cotangent,
    norm_gain,
    w_up,
    w_down,
    gram_left,
    gram_right,
    root_left,
    root_right,
    owner_slot,
    eighth,
    refresh_phase,
):
    low, f32 = jnp.bfloat16, jnp.float32
    section_no = lax.axis_index("section")
    dp_no = lax.axis_index("dp")
    mp_no = lax.axis_index("mp")
    dp_count = lax.axis_size("dp")
    mp_count = lax.axis_size("mp")
    micro_count, row_count, model_width = activations.shape
    rows = micro_count * row_count
    tokens = rows * dp_count
    up, down = w_up[0], w_down[0]
    width, shard_ff = up.shape
    is_first = section_no == 0
    gain = lax.dynamic_slice_in_dim(norm_gain[0], dp_no * width, width)

    block_cols = model_width // BLK
    block_rows = shard_ff // BLK
    group = block_rows * block_cols
    per_dev = gram_left.shape[1]
    pick = lambda table: lax.dynamic_slice_in_dim(
        lax.dynamic_index_in_dim(table, section_no, 0, keepdims=False), mp_no * block_rows, block_rows, 0
    ).reshape(-1)
    slots = (dp_no * mp_count + mp_no) * per_dev + jnp.arange(per_dev, dtype=jnp.int32)
    owned = pick(owner_slot)[None, :] == slots[:, None]
    block = jnp.sum(jnp.where(owned, jnp.arange(group, dtype=jnp.int32)[None, :], 0), axis=1)
    is_due = pick(eighth) == refresh_phase[0] % 8
    due = jnp.sum(jnp.where(owned & is_due[None, :], 1, 0), axis=1).astype(jnp.int32)

    mine = jnp.where(is_first, activations, cotangent).reshape(rows, dp_count, width)
    (start,) = swap_slots(0, [mine.transpose(1, 0, 2)], "dp")
    start_flat = start.reshape(tokens, width)

    def gained(flat):
        return (flat.astype(f32) * gain).astype(low)

    def row_squares(flat):
        values = flat.astype(f32)
        return jnp.sum(values * values, axis=-1).reshape(dp_count, rows)

    product = lax.cond(
        is_first,
        lambda: matmul(gained(start_flat), up).astype(low),
        lambda: matmul(start_flat, down).astype(low),
    )
    summed_a, squares = reduce_dp(
        1, product.reshape(dp_count, rows, shard_ff), row_squares(start_flat)
    )
    inverse_rms = lax.rsqrt(squares / model_width + norm_epsilon)
    hidden = jax.nn.silu(summed_a * inverse_rms[:, None]).astype(low)
    (hidden_a,) = gather_dp(3, [hidden])
    hidden_a = hidden_a.reshape(tokens, shard_ff)
    branch = matmul(hidden_a, down, 1, 1).astype(low)
    share = tokens // mp_count
    (branch,) = reduce_mp(4, [branch.reshape(mp_count, share, width)])
    own_rows = lambda flat: lax.dynamic_slice_in_dim(flat, mp_no * share, share, 0)
    start_own = own_rows(start_flat).astype(f32)
    output = (start_own + branch).astype(low)
    (relayed,) = gather_across(5, [output])
    relayed = relayed.reshape(tokens, width)

    product = matmul(gained(relayed), up).astype(low)
    summed_b, squares = reduce_dp(
        6, product.reshape(dp_count, rows, shard_ff), row_squares(relayed)
    )
    inverse_rms = lax.rsqrt(squares / model_width + norm_epsilon)
    pre_act = summed_b * inverse_rms[:, None]
    hidden = jax.nn.silu(pre_act).astype(low)
    grad_pre = (summed_a * silu_slope(pre_act)).astype(low)
    row_dot = jnp.sum(summed_b * grad_pre.astype(f32), axis=-1)
    side = jnp.concatenate(
        [
            jnp.broadcast_to(inverse_rms[None], (8, rows)),
            jnp.broadcast_to(row_dot[None], (8, rows)),
        ]
    )
    grad_pre, hidden_b, side = gather_dp(8, [grad_pre, hidden, side])
    inverse_rms = side[:, :, 0].reshape(tokens)
    row_dot = side[:, :, 8].reshape(mp_count, share)
    grad_normed = matmul(grad_pre.reshape(tokens, shard_ff), up, 1, 1).astype(low)
    grad_normed, row_dot = reduce_mp(
        9,
        [
            grad_normed.reshape(mp_count, share, width),
            jnp.broadcast_to(row_dot[:, None], (mp_count, 8, share)),
        ],
    )
    row_dot = row_dot[0][:, None]
    inverse_rms = own_rows(inverse_rms)[:, None]
    values = own_rows(relayed).astype(f32)
    grad_values = inverse_rms * (
        gain * grad_normed - values * (inverse_rms * inverse_rms * row_dot / model_width)
    )
    grad_input = (start_own + grad_values).astype(low)
    (grad_relayed,) = gather_across(10, [grad_input])
    grad_out = jnp.where(is_first, grad_relayed.reshape(tokens, width), start_flat)
    (grads,) = gather_dp(11, [grad_out])
    hidden_all = jnp.where(is_first, hidden_a, hidden_b.reshape(tokens, shard_ff))

    results = precondition(
        block // block_cols,
        block % block_cols,
        due,
        hidden_all,
        grads.reshape(dp_count, tokens, width),
        gram_left[0],
        gram_right[0],
        root_left[0],
        root_right[0],
    )
    return tuple(result[None] for result in results)


def solution(mesh):
    return jax.shard_map(
        on_device,
        mesh=mesh,
        in_specs=(
            P(None, "dp", None),
            P(None, "dp", None),
            P("section", None),
            P("section", "dp", "mp"),
            P("section", "dp", "mp"),
            P("section", ("dp", "mp"), None, None),
            P("section", ("dp", "mp"), None, None),
            P("section", ("dp", "mp"), None, None),
            P("section", ("dp", "mp"), None, None),
            P(),
            P(),
            P(),
        ),
        out_specs=(
            P("section", ("dp", "mp"), None, None),
            P("section", ("dp", "mp"), None, None),
            P("section", ("dp", "mp"), None, None),
            P("section", ("dp", "mp"), None, None),
            P("section", ("dp", "mp"), None, None),
        ),
        check_vma=False,
    )
```

```python
import math

import jax
import jax.numpy as jnp
from jax import lax
from jax.experimental import pallas as pl
from jax.experimental.pallas import tpu as pltpu
from jax.sharding import PartitionSpec as P

BLK = 512
MESH = pl.DeviceIdType.MESH
VMEM_LIMIT = 60 * 1024 * 1024

norm_epsilon = 1e-05
decay_rate = 0.9
ridge_shift = 0.001


def meet(devices):
    barrier = pltpu.get_barrier_semaphore()
    for device in devices:
        pl.semaphore_signal(barrier, inc=1, device_id=device, device_id_type=MESH)
    pl.semaphore_wait(barrier, len(devices))


def exchange(collective_id, srcs, out_lead, drop_lead, plan):
    count = len(srcs)
    with_keep = plan.keeps
    copy_total = plan.copies * count

    def kernel(*refs):
        ins, outs = refs[:count], refs[count : 2 * count]
        send_sem, recv_sem, keep_sem = refs[2 * count :]
        items, keep = plan()
        meet([device for _, _, device in items])
        copies = []
        for item_no, (src_index, dst_index, device) in enumerate(items):
            for part_no in range(count):
                at = item_no * count + part_no
                copy = pltpu.make_async_remote_copy(
                    src_ref=ins[part_no].at[src_index],
                    dst_ref=outs[part_no].at[dst_index],
                    send_sem=send_sem.at[at],
                    recv_sem=recv_sem.at[at],
                    device_id=device,
                    device_id_type=MESH,
                )
                copy.start()
                copies.append(copy)
        kept = []
        if with_keep:
            for part_no in range(count):
                copy = pltpu.make_async_copy(
                    ins[part_no].at[keep[0]], outs[part_no].at[keep[1]], keep_sem.at[part_no]
                )
                copy.start()
                kept.append(copy)
        for copy in kept + copies:
            copy.wait()

    return pl.pallas_call(
        kernel,
        out_shape=[
            jax.ShapeDtypeStruct(out_lead + src.shape[drop_lead:], src.dtype) for src in srcs
        ],
        in_specs=[pl.BlockSpec(memory_space=pltpu.VMEM)] * count,
        out_specs=[pl.BlockSpec(memory_space=pl.ANY)] * count,
        scratch_shapes=[
            pltpu.SemaphoreType.DMA((copy_total,)),
            pltpu.SemaphoreType.DMA((copy_total,)),
            pltpu.SemaphoreType.DMA((count,)),
        ],
        compiler_params=pltpu.CompilerParams(
            collective_id=collective_id, has_side_effects=True, vmem_limit_bytes=VMEM_LIMIT
        ),
    )(*srcs)


class Plan:
    def __init__(self, copies, keeps, build):
        self.copies, self.keeps, self.build = copies, keeps, build

    def __call__(self):
        return self.build()


def swap_slots(collective_id, srcs, axis):
    size = lax.axis_size(axis)

    def build():
        me = lax.axis_index(axis)
        items = []
        for step in range(1, size):
            other = lax.rem(me + step, size)
            items.append(((other,), (me,), {axis: other}))
        return items, ((me,), (me,))

    return exchange(collective_id, srcs, (size,), 1, Plan(size - 1, True, build))


def scatter_slots(collective_id, srcs, axis, stride=1):
    size = lax.axis_size(axis) // stride

    def build():
        position = lax.axis_index(axis)
        me, rest = position // stride, lax.rem(position, stride)
        items = []
        for step in range(1, size):
            other = lax.rem(me + step, size)
            items.append(((other,), (step - 1,), {axis: other * stride + rest}))
        return items, None

    return exchange(collective_id, srcs, (size - 1,), 1, Plan(size - 1, False, build))


def pair_half(collective_id, srcs):
    chips = lax.axis_size("dp") // 2

    def build():
        me = lax.axis_index("dp")
        core = lax.rem(me, 2)
        other = 1 - core
        return [((slice(None), other), (slice(None),), {"dp": me - core + other})], None

    return exchange(collective_id, srcs, (chips,), 2, Plan(1, False, build))


def gather_parts(refs_in, refs_out, sems):
    away_send, away_recv, pair_send, pair_recv, keep_sem = sems
    chips = lax.axis_size("dp") // 2
    position = lax.axis_index("dp")
    chip, core = position // 2, lax.rem(position, 2)
    partner = {"dp": chip * 2 + 1 - core}
    others = [lax.rem(chip + step, chips) for step in range(1, chips)]
    parts = []
    for ref_in, ref_out in zip(refs_in, refs_out):
        pieces = pieces_of(ref_in.shape[0])
        for piece in range(pieces):
            size = ref_in.shape[0] // pieces
            parts.append((ref_in, ref_out, pl.ds(piece * size, size)))
    count = len(parts)

    def away_copy(step, part_no):
        ref_in, ref_out, window = parts[part_no]
        at = (step - 1) * count + part_no
        return pltpu.make_async_remote_copy(
            src_ref=ref_in.at[window],
            dst_ref=ref_out.at[chip, core, window],
            send_sem=away_send.at[at],
            recv_sem=away_recv.at[at],
            device_id={"dp": others[step - 1] * 2 + core},
            device_id_type=MESH,
        )

    def pair_copy(step, part_no):
        ref_in, ref_out, window = parts[part_no]
        source = lax.rem(chip + chips - step, chips)
        at = step * count + part_no
        return pltpu.make_async_remote_copy(
            src_ref=ref_in.at[window] if step == 0 else ref_out.at[source, core, window],
            dst_ref=ref_out.at[source, core, window],
            send_sem=pair_send.at[at],
            recv_sem=pair_recv.at[at],
            device_id=partner,
            device_id_type=MESH,
        )

    def keep_copy(part_no):
        ref_in, ref_out, window = parts[part_no]
        return pltpu.make_async_copy(
            ref_in.at[window], ref_out.at[chip, core, window], keep_sem.at[part_no]
        )

    def begin():
        for part_no in range(count):
            for step in range(1, chips):
                away_copy(step, part_no).start()
        for part_no in range(count):
            pair_copy(0, part_no).start()
            keep_copy(part_no).start()

    def finish():
        for part_no in range(count):
            for step in range(1, chips):
                away_copy(step, part_no).wait_recv()
                pair_copy(step, part_no).start()
        for part_no in range(count):
            keep_copy(part_no).wait()
            for step in range(1, chips):
                away_copy(step, part_no).wait_send()
            for step in range(chips):
                pair_copy(step, part_no).wait()

    return [partner] + [{"dp": other * 2 + core} for other in others], begin, finish


def pieces_of(rows):
    return 4 if rows % 64 == 0 else 1


def gather_shapes(srcs):
    chips = lax.axis_size("dp") // 2
    count = sum(pieces_of(src.shape[0]) for src in srcs)
    dma = pltpu.SemaphoreType.DMA
    return (
        [jax.ShapeDtypeStruct((chips, 2) + src.shape, src.dtype) for src in srcs],
        [
            dma(((chips - 1) * count,)),
            dma(((chips - 1) * count,)),
            dma((chips * count,)),
            dma((chips * count,)),
            dma((count,)),
        ],
    )


def gather_dp(collective_id, srcs):
    count = len(srcs)
    shapes, sems = gather_shapes(srcs)

    def kernel(*refs):
        greet, begin, finish = gather_parts(
            refs[:count], refs[count : 2 * count], refs[2 * count :]
        )
        meet(greet)
        begin()
        finish()

    return pl.pallas_call(
        kernel,
        out_shape=shapes,
        in_specs=[pl.BlockSpec(memory_space=pltpu.VMEM)] * count,
        out_specs=[pl.BlockSpec(memory_space=pl.ANY)] * count,
        scratch_shapes=sems,
        compiler_params=pltpu.CompilerParams(
            collective_id=collective_id, has_side_effects=True, vmem_limit_bytes=VMEM_LIMIT
        ),
    )(*srcs)


def relay(collective_id, sender, product, operands, finish_rows, side=None, aside=None):
    size, share, width = product.shape
    pieces = pieces_of(share)
    rows = share // pieces
    operand_total = len(operands)
    has_side, has_aside = side is not None, aside is not None
    hops = size - 1
    aside_shapes, aside_sems = gather_shapes([aside]) if has_aside else ([], [])

    def kernel(*refs):
        refs = list(refs)
        take = lambda n: [refs.pop(0) for _ in range(n)]
        (product_ref,) = take(1)
        operand_refs = take(operand_total)
        side_ref = take(1)[0] if has_side else None
        aside_in = take(1) if has_aside else []
        (out_ref,) = take(1)
        aside_out = take(1) if has_aside else []
        landed, ready = take(2)
        side_landed = take(1)[0] if has_side else None
        sum_send, sum_recv, far_send, far_recv, side_send, side_recv = take(6)
        me = lax.axis_index("mp")
        section = lax.axis_index("section")
        far = 1 - section
        ring = [lax.rem(me + step, size) for step in range(size)]
        greet = [{"mp": ring[step]} for step in range(1, size)]
        greet += [{"section": far, "mp": other} for other in ring]
        if has_aside:
            aside_greet, begin, finish = gather_parts(aside_in, aside_out, refs)
            greet += aside_greet
        meet(greet)

        def sum_copy(piece, step):
            window = pl.ds(piece * rows, rows)
            at = piece * hops + step - 1
            return pltpu.make_async_remote_copy(
                src_ref=product_ref.at[ring[step], window],
                dst_ref=landed.at[step - 1, window],
                send_sem=sum_send.at[at],
                recv_sem=sum_recv.at[at],
                device_id={"mp": ring[step]},
                device_id_type=MESH,
            )

        def side_copy(step):
            return pltpu.make_async_remote_copy(
                src_ref=side_ref.at[ring[step]],
                dst_ref=side_landed.at[step - 1],
                send_sem=side_send.at[step - 1],
                recv_sem=side_recv.at[step - 1],
                device_id={"mp": ring[step]},
                device_id_type=MESH,
            )

        def far_copy(piece, step):
            at = piece * size + step
            window = pl.ds(piece * rows, rows)
            return pltpu.make_async_remote_copy(
                src_ref=ready.at[window],
                dst_ref=out_ref.at[me, window],
                send_sem=far_send.at[at],
                recv_sem=far_recv.at[at],
                device_id={"section": far, "mp": ring[step]},
                device_id_type=MESH,
            )

        @pl.when(section == sender)
        def _():
            if has_side:
                for step in range(1, size):
                    side_copy(step).start()
            for piece in range(pieces):
                for step in range(1, size):
                    sum_copy(piece, step).start()
            if has_aside:
                begin()
            if has_side:
                for step in range(1, size):
                    side_copy(step).wait()
            for piece in range(pieces):
                for step in range(1, size):
                    sum_copy(piece, step).wait_recv()
                window = pl.ds(piece * rows, rows)
                total = product_ref[me, window, :].astype(jnp.float32)
                for step in range(1, size):
                    total += landed[step - 1, window, :].astype(jnp.float32)
                side_total = None
                if has_side:
                    side_total = side_ref[me, window, :].astype(jnp.float32)
                    for step in range(1, size):
                        side_total += side_landed[step - 1, window, :].astype(jnp.float32)
                cut = [
                    ref[window, :] if ref.shape[0] == share else ref[...] for ref in operand_refs
                ]
                ready[window, :] = finish_rows(total, side_total, *cut).astype(ready.dtype)
                for step in range(size):
                    far_copy(piece, step).start()
            if has_aside:
                finish()
            for piece in range(pieces):
                for step in range(1, size):
                    sum_copy(piece, step).wait_send()
                for step in range(size):
                    far_copy(piece, step).wait_send()

        @pl.when(section != sender)
        def _():
            for piece in range(pieces):
                for step in range(size):
                    far_copy(piece, step).wait_recv()

    dma = pltpu.SemaphoreType.DMA
    inputs = [product] + list(operands) + [x for x in (side, aside) if x is not None]
    return pl.pallas_call(
        kernel,
        out_shape=[jax.ShapeDtypeStruct(product.shape, jnp.bfloat16)] + aside_shapes,
        in_specs=[pl.BlockSpec(memory_space=pltpu.VMEM)] * len(inputs),
        out_specs=[pl.BlockSpec(memory_space=pl.ANY)] * (1 + len(aside_shapes)),
        scratch_shapes=[
            pltpu.VMEM((hops, share, width), product.dtype),
            pltpu.VMEM((share, width), jnp.bfloat16),
        ]
        + ([pltpu.VMEM((hops,) + side.shape[1:], side.dtype)] if has_side else [])
        + [
            dma((pieces * hops,)),
            dma((pieces * hops,)),
            dma((pieces * size,)),
            dma((pieces * size,)),
            dma((hops,)),
            dma((hops,)),
        ]
        + aside_sems,
        compiler_params=pltpu.CompilerParams(
            collective_id=collective_id, has_side_effects=True, vmem_limit_bytes=VMEM_LIMIT
        ),
    )(*inputs)


def reduce_dp(first_id, product, row_sums):
    total, rows, columns = product.shape
    chips = total // 2
    position = lax.axis_index("dp")
    chip, core = position // 2, position % 2
    parts = [
        product.reshape(chips, 2, rows, columns),
        jnp.broadcast_to(row_sums[:, None, :], (total, 8, rows)).reshape(chips, 2, 8, rows),
    ]
    received = pair_half(first_id, parts)
    halves = [
        (
            lax.dynamic_index_in_dim(part, core, 1, keepdims=False).astype(jnp.float32)
            + other.astype(jnp.float32)
        ).astype(part.dtype)
        for part, other in zip(parts, received)
    ]
    received = scatter_slots(first_id + 1, halves, "dp", 2)
    summed = [
        lax.dynamic_index_in_dim(half, chip, 0, keepdims=False).astype(jnp.float32)
        + jnp.sum(other.astype(jnp.float32), axis=0)
        for half, other in zip(halves, received)
    ]
    return summed[0], summed[1][0]


def silu_slope(pre_act):
    sigmoid_values = jax.nn.sigmoid(pre_act)
    return sigmoid_values * (1.0 + pre_act * (1.0 - sigmoid_values))


def matmul(left, right, left_dim=1, right_dim=0):
    return lax.dot_general(
        left, right, (((left_dim,), (right_dim,)), ((), ())), preferred_element_type=jnp.float32
    )


def inverse_root(matrix):
    low = jnp.bfloat16
    order = matrix.shape[-1]
    on_diagonal = lax.broadcasted_iota(jnp.int32, (order, order), 0) == lax.broadcasted_iota(
        jnp.int32, (order, order), 1
    )
    identity = jnp.where(on_diagonal, 1.0, 0.0).astype(jnp.float32)
    shifted = matrix + ridge_shift * identity
    norm_sq = jnp.sum(jnp.sum(shifted * shifted, axis=1, keepdims=True), axis=0, keepdims=True)
    factor = 2.5 / jnp.sqrt(norm_sq)
    moment = factor * shifted
    moment_low = moment.astype(low)
    moment_sq = matmul(moment_low, moment_low)
    square = (1.5625 * identity - 0.625 * moment + 0.0625 * moment_sq).astype(low)
    stepped = (1.25 * moment - 0.25 * moment_sq).astype(low)
    third = matmul(square, stepped).astype(low)
    fifth = matmul(square, third)
    scale = jnp.sqrt(jnp.sqrt(factor))
    return scale * (1.5625 * identity - 0.3125 * moment - 0.25 * fifth)


def precondition(block_row, block_col, due, hidden, grads, gram_l, gram_r, root_l, root_r):
    slots = gram_l.shape[0]
    tokens = hidden.shape[0]
    width = grads.shape[2]
    scale = 1.0 / math.sqrt(tokens)

    def kernel(
        row_ref, col_ref, due_ref, hid_ref, grad_ref, gl_ref, gr_ref, rl_ref, rr_ref,
        gl_out, gr_out, rl_out, rr_out, up_out,
    ):
        slot = pl.program_id(0)
        pieces = [grad_ref[piece] for piece in range(grad_ref.shape[0])]
        dy = pieces[0] if len(pieces) == 1 else jnp.concatenate(pieces, axis=1)
        grad_low = (matmul(hid_ref[...], dy, 0, 0) * scale).astype(jnp.bfloat16)
        gl_out[0] = decay_rate * gl_ref[0] + matmul(grad_low, grad_low, 1, 1) * (1.0 / BLK)
        gr_out[0] = decay_rate * gr_ref[0] + matmul(grad_low, grad_low, 0, 0) * (1.0 / BLK)

        @pl.when(due_ref[slot] != 0)
        def _():
            rl_out[0] = inverse_root(gl_out[0]).astype(jnp.bfloat16)
            rr_out[0] = inverse_root(gr_out[0]).astype(jnp.bfloat16)

        @pl.when(due_ref[slot] == 0)
        def _():
            rl_out[0] = rl_ref[0]
            rr_out[0] = rr_ref[0]

        right_part = matmul(grad_low, rr_out[0]).astype(jnp.bfloat16)
        up_out[0] = matmul(rl_out[0], right_part).astype(jnp.bfloat16)

    if width >= BLK:
        per = width // BLK
        grad_spec = pl.BlockSpec(
            (1, tokens, BLK),
            lambda s, row, col, due: (lax.div(col[s], per), 0, lax.rem(col[s], per)),
        )
    else:
        grad_spec = pl.BlockSpec(
            (BLK // width, tokens, width), lambda s, row, col, due: (col[s], 0, 0)
        )
    square_spec = pl.BlockSpec((1, BLK, BLK), lambda s, row, col, due: (s, 0, 0))
    return pl.pallas_call(
        kernel,
        grid_spec=pltpu.PrefetchScalarGridSpec(
            num_scalar_prefetch=3,
            grid=(slots,),
            in_specs=[
                pl.BlockSpec((tokens, BLK), lambda s, row, col, due: (0, row[s])),
                grad_spec,
            ]
            + [square_spec] * 4,
            out_specs=[square_spec] * 5,
        ),
        out_shape=[
            jax.ShapeDtypeStruct(gram_l.shape, jnp.float32),
            jax.ShapeDtypeStruct(gram_l.shape, jnp.float32),
            jax.ShapeDtypeStruct(gram_l.shape, jnp.bfloat16),
            jax.ShapeDtypeStruct(gram_l.shape, jnp.bfloat16),
            jax.ShapeDtypeStruct(gram_l.shape, jnp.bfloat16),
        ],
        compiler_params=pltpu.CompilerParams(
            dimension_semantics=("arbitrary",), vmem_limit_bytes=VMEM_LIMIT
        ),
    )(block_row, block_col, due, hidden, grads, gram_l, gram_r, root_l, root_r)


def on_device(
    activations,
    cotangent,
    norm_gain,
    w_up,
    w_down,
    gram_left,
    gram_right,
    root_left,
    root_right,
    owner_slot,
    eighth,
    refresh_phase,
):
    low, f32 = jnp.bfloat16, jnp.float32
    section_no = lax.axis_index("section")
    dp_no = lax.axis_index("dp")
    mp_no = lax.axis_index("mp")
    dp_count = lax.axis_size("dp")
    mp_count = lax.axis_size("mp")
    micro_count, row_count, model_width = activations.shape
    rows = micro_count * row_count
    tokens = rows * dp_count
    up, down = w_up[0], w_down[0]
    width, shard_ff = up.shape
    is_first = section_no == 0
    gain = lax.dynamic_slice_in_dim(norm_gain[0], dp_no * width, width)

    block_cols = model_width // BLK
    block_rows = shard_ff // BLK
    group = block_rows * block_cols
    per_dev = gram_left.shape[1]
    pick = lambda table: lax.dynamic_slice_in_dim(
        lax.dynamic_index_in_dim(table, section_no, 0, keepdims=False), mp_no * block_rows, block_rows, 0
    ).reshape(-1)
    slots = (dp_no * mp_count + mp_no) * per_dev + jnp.arange(per_dev, dtype=jnp.int32)
    owned = pick(owner_slot)[None, :] == slots[:, None]
    block = jnp.sum(jnp.where(owned, jnp.arange(group, dtype=jnp.int32)[None, :], 0), axis=1)
    is_due = pick(eighth) == refresh_phase[0] % 8
    due = jnp.sum(jnp.where(owned & is_due[None, :], 1, 0), axis=1).astype(jnp.int32)

    mine = jnp.where(is_first, activations, cotangent).reshape(rows, dp_count, width)
    (start,) = swap_slots(0, [mine.transpose(1, 0, 2)], "dp")
    start_flat = start.reshape(tokens, width)

    def gained(flat):
        return (flat.astype(f32) * gain).astype(low)

    def row_squares(flat):
        values = flat.astype(f32)
        return jnp.sum(values * values, axis=-1).reshape(dp_count, rows)

    product = lax.cond(
        is_first,
        lambda: matmul(gained(start_flat), up).astype(low),
        lambda: matmul(start_flat, down).astype(low),
    )
    summed_a, squares = reduce_dp(
        1, product.reshape(dp_count, rows, shard_ff), row_squares(start_flat)
    )
    inverse_rms = lax.rsqrt(squares / model_width + norm_epsilon)
    hidden = jax.nn.silu(summed_a * inverse_rms[:, None]).astype(low)
    (hidden_a,) = gather_dp(3, [hidden])
    hidden_a = hidden_a.reshape(tokens, shard_ff)
    branch = matmul(hidden_a, down, 1, 1).astype(low)
    share = tokens // mp_count
    own_rows = lambda flat: lax.dynamic_slice_in_dim(flat, mp_no * share, share, 0)
    start_own = own_rows(start_flat)
    (relayed,) = relay(
        4,
        0,
        branch.reshape(mp_count, share, width),
        [start_own],
        lambda total, side, base: base.astype(f32) + total,
    )
    relayed = relayed.reshape(tokens, width)

    product = matmul(gained(relayed), up).astype(low)
    summed_b, squares = reduce_dp(
        6, product.reshape(dp_count, rows, shard_ff), row_squares(relayed)
    )
    inverse_rms = lax.rsqrt(squares / model_width + norm_epsilon)
    pre_act = summed_b * inverse_rms[:, None]
    hidden = jax.nn.silu(pre_act).astype(low)
    grad_pre = (summed_a * silu_slope(pre_act)).astype(low)
    row_dot = jnp.sum(summed_b * grad_pre.astype(f32), axis=-1)
    side = jnp.concatenate(
        [
            jnp.broadcast_to(inverse_rms[None], (8, rows)),
            jnp.broadcast_to(row_dot[None], (8, rows)),
        ]
    )
    grad_pre, side = gather_dp(8, [grad_pre, side])
    inverse_rms = own_rows(side[:, :, 0].reshape(tokens))[:, None]
    row_dot = side[:, :, 8].reshape(tokens, 1)
    dot_high = row_dot.astype(low)
    dot_low = (row_dot - lax.optimization_barrier(dot_high).astype(f32)).astype(low)
    dots = jnp.where(jnp.arange(128)[None, :] < 64, dot_high, dot_low)
    grad_normed = matmul(grad_pre.reshape(tokens, shard_ff), up, 1, 1).astype(low)
    spread = lambda column: jnp.broadcast_to(column, (share, 128))

    def input_gradient(total, side, base, values, rms, cubed, gain_row):
        row_dot = side[:, 0:1] + side[:, 64:65]
        return base.astype(f32) + (
            rms[:, 0:1] * (gain_row * total)
            - values.astype(f32) * (cubed[:, 0:1] * row_dot)
        )

    grad_relayed, hidden_b = relay(
        9,
        1,
        grad_normed.reshape(mp_count, share, width),
        [
            start_own,
            own_rows(relayed),
            spread(inverse_rms),
            spread(inverse_rms * inverse_rms * inverse_rms / model_width),
            gain[None],
        ],
        input_gradient,
        side=dots.reshape(mp_count, share, 128),
        aside=hidden,
    )
    grad_out = jnp.where(is_first, grad_relayed.reshape(tokens, width), start_flat)
    (grads,) = gather_dp(11, [grad_out])
    hidden_all = jnp.where(is_first, hidden_a, hidden_b.reshape(tokens, shard_ff))

    results = precondition(
        block // block_cols,
        block % block_cols,
        due,
        hidden_all,
        grads.reshape(dp_count, tokens, width),
        gram_left[0],
        gram_right[0],
        root_left[0],
        root_right[0],
    )
    return tuple(result[None] for result in results)


def solution(mesh):
    return jax.shard_map(
        on_device,
        mesh=mesh,
        in_specs=(
            P(None, "dp", None),
            P(None, "dp", None),
            P("section", None),
            P("section", "dp", "mp"),
            P("section", "dp", "mp"),
            P("section", ("dp", "mp"), None, None),
            P("section", ("dp", "mp"), None, None),
            P("section", ("dp", "mp"), None, None),
            P("section", ("dp", "mp"), None, None),
            P(),
            P(),
            P(),
        ),
        out_specs=(
            P("section", ("dp", "mp"), None, None),
            P("section", ("dp", "mp"), None, None),
            P("section", ("dp", "mp"), None, None),
            P("section", ("dp", "mp"), None, None),
            P("section", ("dp", "mp"), None, None),
        ),
        check_vma=False,
    )
```

```python
import math

import jax
import jax.numpy as jnp
from jax import lax
from jax.experimental import pallas as pl
from jax.experimental.pallas import tpu as pltpu
from jax.sharding import PartitionSpec as P

BLK = 512
MESH = pl.DeviceIdType.MESH
VMEM_LIMIT = 60 * 1024 * 1024

norm_epsilon = 1e-05
decay_rate = 0.9
ridge_shift = 0.001


def meet(devices):
    barrier = pltpu.get_barrier_semaphore()
    for device in devices:
        pl.semaphore_signal(barrier, inc=1, device_id=device, device_id_type=MESH)
    pl.semaphore_wait(barrier, len(devices))


def exchange(collective_id, srcs, out_lead, drop_lead, plan):
    count = len(srcs)
    with_keep = plan.keeps
    copy_total = plan.copies * count

    def kernel(*refs):
        ins, outs = refs[:count], refs[count : 2 * count]
        send_sem, recv_sem, keep_sem = refs[2 * count :]
        items, keep = plan()
        meet([device for _, _, device in items])
        copies = []
        for item_no, (src_index, dst_index, device) in enumerate(items):
            for part_no in range(count):
                at = item_no * count + part_no
                copy = pltpu.make_async_remote_copy(
                    src_ref=ins[part_no].at[src_index],
                    dst_ref=outs[part_no].at[dst_index],
                    send_sem=send_sem.at[at],
                    recv_sem=recv_sem.at[at],
                    device_id=device,
                    device_id_type=MESH,
                )
                copy.start()
                copies.append(copy)
        kept = []
        if with_keep:
            for part_no in range(count):
                copy = pltpu.make_async_copy(
                    ins[part_no].at[keep[0]], outs[part_no].at[keep[1]], keep_sem.at[part_no]
                )
                copy.start()
                kept.append(copy)
        for copy in kept + copies:
            copy.wait()

    return pl.pallas_call(
        kernel,
        out_shape=[
            jax.ShapeDtypeStruct(out_lead + src.shape[drop_lead:], src.dtype) for src in srcs
        ],
        in_specs=[pl.BlockSpec(memory_space=pltpu.VMEM)] * count,
        out_specs=[pl.BlockSpec(memory_space=pl.ANY)] * count,
        scratch_shapes=[
            pltpu.SemaphoreType.DMA((copy_total,)),
            pltpu.SemaphoreType.DMA((copy_total,)),
            pltpu.SemaphoreType.DMA((count,)),
        ],
        compiler_params=pltpu.CompilerParams(
            collective_id=collective_id, has_side_effects=True, vmem_limit_bytes=VMEM_LIMIT
        ),
    )(*srcs)


class Plan:
    def __init__(self, copies, keeps, build):
        self.copies, self.keeps, self.build = copies, keeps, build

    def __call__(self):
        return self.build()


def swap_slots(collective_id, srcs, axis):
    size = lax.axis_size(axis)

    def build():
        me = lax.axis_index(axis)
        items = []
        for step in range(1, size):
            other = lax.rem(me + step, size)
            items.append(((other,), (me,), {axis: other}))
        return items, ((me,), (me,))

    return exchange(collective_id, srcs, (size,), 1, Plan(size - 1, True, build))


def scatter_slots(collective_id, srcs, axis, stride=1):
    size = lax.axis_size(axis) // stride

    def build():
        position = lax.axis_index(axis)
        me, rest = position // stride, lax.rem(position, stride)
        items = []
        for step in range(1, size):
            other = lax.rem(me + step, size)
            items.append(((other,), (step - 1,), {axis: other * stride + rest}))
        return items, None

    return exchange(collective_id, srcs, (size - 1,), 1, Plan(size - 1, False, build))


def pair_half(collective_id, srcs):
    chips = lax.axis_size("dp") // 2

    def build():
        me = lax.axis_index("dp")
        core = lax.rem(me, 2)
        other = 1 - core
        return [((slice(None), other), (slice(None),), {"dp": me - core + other})], None

    return exchange(collective_id, srcs, (chips,), 2, Plan(1, False, build))


def gather_parts(refs_in, refs_out, sems):
    away_send, away_recv, pair_send, pair_recv, keep_sem = sems
    chips = lax.axis_size("dp") // 2
    position = lax.axis_index("dp")
    chip, core = position // 2, lax.rem(position, 2)
    partner = {"dp": chip * 2 + 1 - core}
    others = [lax.rem(chip + step, chips) for step in range(1, chips)]
    parts = []
    for ref_in, ref_out in zip(refs_in, refs_out):
        pieces = pieces_of(ref_in.shape[0])
        for piece in range(pieces):
            size = ref_in.shape[0] // pieces
            parts.append((ref_in, ref_out, pl.ds(piece * size, size)))
    count = len(parts)

    def away_copy(step, part_no):
        ref_in, ref_out, window = parts[part_no]
        at = (step - 1) * count + part_no
        return pltpu.make_async_remote_copy(
            src_ref=ref_in.at[window],
            dst_ref=ref_out.at[chip, core, window],
            send_sem=away_send.at[at],
            recv_sem=away_recv.at[at],
            device_id={"dp": others[step - 1] * 2 + core},
            device_id_type=MESH,
        )

    def pair_copy(step, part_no):
        ref_in, ref_out, window = parts[part_no]
        source = lax.rem(chip + chips - step, chips)
        at = step * count + part_no
        return pltpu.make_async_remote_copy(
            src_ref=ref_in.at[window] if step == 0 else ref_out.at[source, core, window],
            dst_ref=ref_out.at[source, core, window],
            send_sem=pair_send.at[at],
            recv_sem=pair_recv.at[at],
            device_id=partner,
            device_id_type=MESH,
        )

    def keep_copy(part_no):
        ref_in, ref_out, window = parts[part_no]
        return pltpu.make_async_copy(
            ref_in.at[window], ref_out.at[chip, core, window], keep_sem.at[part_no]
        )

    def begin():
        for part_no in range(count):
            for step in range(1, chips):
                away_copy(step, part_no).start()
        for part_no in range(count):
            pair_copy(0, part_no).start()
            keep_copy(part_no).start()

    def finish():
        for part_no in range(count):
            for step in range(1, chips):
                away_copy(step, part_no).wait_recv()
                pair_copy(step, part_no).start()
        for part_no in range(count):
            keep_copy(part_no).wait()
            for step in range(1, chips):
                away_copy(step, part_no).wait_send()
            for step in range(chips):
                pair_copy(step, part_no).wait()

    return [partner] + [{"dp": other * 2 + core} for other in others], begin, finish


def pieces_of(rows):
    return 4 if rows % 64 == 0 else 1


def gather_shapes(srcs):
    chips = lax.axis_size("dp") // 2
    count = sum(pieces_of(src.shape[0]) for src in srcs)
    dma = pltpu.SemaphoreType.DMA
    return (
        [jax.ShapeDtypeStruct((chips, 2) + src.shape, src.dtype) for src in srcs],
        [
            dma(((chips - 1) * count,)),
            dma(((chips - 1) * count,)),
            dma((chips * count,)),
            dma((chips * count,)),
            dma((count,)),
        ],
    )


def gather_dp(collective_id, srcs):
    count = len(srcs)
    shapes, sems = gather_shapes(srcs)

    def kernel(*refs):
        greet, begin, finish = gather_parts(
            refs[:count], refs[count : 2 * count], refs[2 * count :]
        )
        meet(greet)
        begin()
        finish()

    return pl.pallas_call(
        kernel,
        out_shape=shapes,
        in_specs=[pl.BlockSpec(memory_space=pltpu.VMEM)] * count,
        out_specs=[pl.BlockSpec(memory_space=pl.ANY)] * count,
        scratch_shapes=sems,
        compiler_params=pltpu.CompilerParams(
            collective_id=collective_id, has_side_effects=True, vmem_limit_bytes=VMEM_LIMIT
        ),
    )(*srcs)


def relay(collective_id, sender, product, operands, finish_rows, side=None, aside=None):
    size, share, width = product.shape
    pieces = pieces_of(share)
    rows = share // pieces
    operand_total = len(operands)
    has_side, has_aside = side is not None, aside is not None
    hops = size - 1
    aside_shapes, aside_sems = gather_shapes([aside]) if has_aside else ([], [])

    def kernel(*refs):
        refs = list(refs)
        take = lambda n: [refs.pop(0) for _ in range(n)]
        (product_ref,) = take(1)
        operand_refs = take(operand_total)
        side_ref = take(1)[0] if has_side else None
        aside_in = take(1) if has_aside else []
        (out_ref,) = take(1)
        aside_out = take(1) if has_aside else []
        landed, ready = take(2)
        side_landed = take(1)[0] if has_side else None
        sum_send, sum_recv, far_send, far_recv, side_send, side_recv = take(6)
        me = lax.axis_index("mp")
        section = lax.axis_index("section")
        far = 1 - section
        ring = [lax.rem(me + step, size) for step in range(size)]
        greet = [{"mp": ring[step]} for step in range(1, size)]
        greet += [{"section": far}]
        if has_aside:
            aside_greet, begin, finish = gather_parts(aside_in, aside_out, refs)
            greet += aside_greet
        meet(greet)

        def sum_copy(piece, step):
            window = pl.ds(piece * rows, rows)
            at = piece * hops + step - 1
            return pltpu.make_async_remote_copy(
                src_ref=product_ref.at[ring[step], window],
                dst_ref=landed.at[step - 1, window],
                send_sem=sum_send.at[at],
                recv_sem=sum_recv.at[at],
                device_id={"mp": ring[step]},
                device_id_type=MESH,
            )

        def side_copy(step):
            return pltpu.make_async_remote_copy(
                src_ref=side_ref.at[ring[step]],
                dst_ref=side_landed.at[step - 1],
                send_sem=side_send.at[step - 1],
                recv_sem=side_recv.at[step - 1],
                device_id={"mp": ring[step]},
                device_id_type=MESH,
            )

        def far_copy(piece):
            at = piece * size
            window = pl.ds(piece * rows, rows)
            return pltpu.make_async_remote_copy(
                src_ref=ready.at[window],
                dst_ref=out_ref.at[me, window],
                send_sem=far_send.at[at],
                recv_sem=far_recv.at[at],
                device_id={"section": far},
                device_id_type=MESH,
            )

        def onward_copy(piece, step):
            at = piece * size + step
            window = pl.ds(piece * rows, rows)
            return pltpu.make_async_remote_copy(
                src_ref=out_ref.at[me, window],
                dst_ref=out_ref.at[me, window],
                send_sem=far_send.at[at],
                recv_sem=far_recv.at[at],
                device_id={"mp": ring[step]},
                device_id_type=MESH,
            )

        @pl.when(section == sender)
        def _():
            if has_side:
                for step in range(1, size):
                    side_copy(step).start()
            for piece in range(pieces):
                for step in range(1, size):
                    sum_copy(piece, step).start()
            if has_aside:
                begin()
            if has_side:
                for step in range(1, size):
                    side_copy(step).wait()
            for piece in range(pieces):
                for step in range(1, size):
                    sum_copy(piece, step).wait_recv()
                window = pl.ds(piece * rows, rows)
                total = product_ref[me, window, :].astype(jnp.float32)
                for step in range(1, size):
                    total += landed[step - 1, window, :].astype(jnp.float32)
                side_total = None
                if has_side:
                    side_total = side_ref[me, window, :].astype(jnp.float32)
                    for step in range(1, size):
                        side_total += side_landed[step - 1, window, :].astype(jnp.float32)
                cut = [
                    ref[window, :] if ref.shape[0] == share else ref[...] for ref in operand_refs
                ]
                ready[window, :] = finish_rows(total, side_total, *cut).astype(ready.dtype)
                far_copy(piece).start()
            if has_aside:
                finish()
            for piece in range(pieces):
                for step in range(1, size):
                    sum_copy(piece, step).wait_send()
                far_copy(piece).wait_send()

        @pl.when(section != sender)
        def _():
            for piece in range(pieces):
                far_copy(piece).wait_recv()
                for step in range(1, size):
                    onward_copy(piece, step).start()
            for piece in range(pieces):
                for step in range(1, size):
                    onward_copy(piece, step).wait()

    dma = pltpu.SemaphoreType.DMA
    inputs = [product] + list(operands) + [x for x in (side, aside) if x is not None]
    return pl.pallas_call(
        kernel,
        out_shape=[jax.ShapeDtypeStruct(product.shape, jnp.bfloat16)] + aside_shapes,
        in_specs=[pl.BlockSpec(memory_space=pltpu.VMEM)] * len(inputs),
        out_specs=[pl.BlockSpec(memory_space=pl.ANY)] * (1 + len(aside_shapes)),
        scratch_shapes=[
            pltpu.VMEM((hops, share, width), product.dtype),
            pltpu.VMEM((share, width), jnp.bfloat16),
        ]
        + ([pltpu.VMEM((hops,) + side.shape[1:], side.dtype)] if has_side else [])
        + [
            dma((pieces * hops,)),
            dma((pieces * hops,)),
            dma((pieces * size,)),
            dma((pieces * size,)),
            dma((hops,)),
            dma((hops,)),
        ]
        + aside_sems,
        compiler_params=pltpu.CompilerParams(
            collective_id=collective_id, has_side_effects=True, vmem_limit_bytes=VMEM_LIMIT
        ),
    )(*inputs)


def reduce_dp(first_id, product, row_sums):
    total, rows, columns = product.shape
    chips = total // 2
    position = lax.axis_index("dp")
    chip, core = position // 2, position % 2
    parts = [
        product.reshape(chips, 2, rows, columns),
        jnp.broadcast_to(row_sums[:, None, :], (total, 8, rows)).reshape(chips, 2, 8, rows),
    ]
    received = pair_half(first_id, parts)
    halves = [
        (
            lax.dynamic_index_in_dim(part, core, 1, keepdims=False).astype(jnp.float32)
            + other.astype(jnp.float32)
        ).astype(part.dtype)
        for part, other in zip(parts, received)
    ]
    received = scatter_slots(first_id + 1, halves, "dp", 2)
    summed = [
        lax.dynamic_index_in_dim(half, chip, 0, keepdims=False).astype(jnp.float32)
        + jnp.sum(other.astype(jnp.float32), axis=0)
        for half, other in zip(halves, received)
    ]
    return summed[0], summed[1][0]


def silu_slope(pre_act):
    sigmoid_values = jax.nn.sigmoid(pre_act)
    return sigmoid_values * (1.0 + pre_act * (1.0 - sigmoid_values))


def matmul(left, right, left_dim=1, right_dim=0):
    return lax.dot_general(
        left, right, (((left_dim,), (right_dim,)), ((), ())), preferred_element_type=jnp.float32
    )


def inverse_root(matrix):
    low = jnp.bfloat16
    order = matrix.shape[-1]
    on_diagonal = lax.broadcasted_iota(jnp.int32, (order, order), 0) == lax.broadcasted_iota(
        jnp.int32, (order, order), 1
    )
    identity = jnp.where(on_diagonal, 1.0, 0.0).astype(jnp.float32)
    shifted = matrix + ridge_shift * identity
    norm_sq = jnp.sum(jnp.sum(shifted * shifted, axis=1, keepdims=True), axis=0, keepdims=True)
    factor = 2.5 / jnp.sqrt(norm_sq)
    moment = factor * shifted
    moment_low = moment.astype(low)
    moment_sq = matmul(moment_low, moment_low)
    square = (1.5625 * identity - 0.625 * moment + 0.0625 * moment_sq).astype(low)
    stepped = (1.25 * moment - 0.25 * moment_sq).astype(low)
    third = matmul(square, stepped).astype(low)
    fifth = matmul(square, third)
    scale = jnp.sqrt(jnp.sqrt(factor))
    return scale * (1.5625 * identity - 0.3125 * moment - 0.25 * fifth)


def precondition(block_row, block_col, due, hidden, grads, gram_l, gram_r, root_l, root_r):
    slots = gram_l.shape[0]
    tokens = hidden.shape[0]
    width = grads.shape[2]
    scale = 1.0 / math.sqrt(tokens)

    def kernel(
        row_ref, col_ref, due_ref, hid_ref, grad_ref, gl_ref, gr_ref, rl_ref, rr_ref,
        gl_out, gr_out, rl_out, rr_out, up_out,
    ):
        slot = pl.program_id(0)
        pieces = [grad_ref[piece] for piece in range(grad_ref.shape[0])]
        dy = pieces[0] if len(pieces) == 1 else jnp.concatenate(pieces, axis=1)
        grad_low = (matmul(hid_ref[...], dy, 0, 0) * scale).astype(jnp.bfloat16)
        gl_out[0] = decay_rate * gl_ref[0] + matmul(grad_low, grad_low, 1, 1) * (1.0 / BLK)
        gr_out[0] = decay_rate * gr_ref[0] + matmul(grad_low, grad_low, 0, 0) * (1.0 / BLK)

        @pl.when(due_ref[slot] != 0)
        def _():
            rl_out[0] = inverse_root(gl_out[0]).astype(jnp.bfloat16)
            rr_out[0] = inverse_root(gr_out[0]).astype(jnp.bfloat16)

        @pl.when(due_ref[slot] == 0)
        def _():
            rl_out[0] = rl_ref[0]
            rr_out[0] = rr_ref[0]

        right_part = matmul(grad_low, rr_out[0]).astype(jnp.bfloat16)
        up_out[0] = matmul(rl_out[0], right_part).astype(jnp.bfloat16)

    if width >= BLK:
        per = width // BLK
        grad_spec = pl.BlockSpec(
            (1, tokens, BLK),
            lambda s, row, col, due: (lax.div(col[s], per), 0, lax.rem(col[s], per)),
        )
    else:
        grad_spec = pl.BlockSpec(
            (BLK // width, tokens, width), lambda s, row, col, due: (col[s], 0, 0)
        )
    square_spec = pl.BlockSpec((1, BLK, BLK), lambda s, row, col, due: (s, 0, 0))
    return pl.pallas_call(
        kernel,
        grid_spec=pltpu.PrefetchScalarGridSpec(
            num_scalar_prefetch=3,
            grid=(slots,),
            in_specs=[
                pl.BlockSpec((tokens, BLK), lambda s, row, col, due: (0, row[s])),
                grad_spec,
            ]
            + [square_spec] * 4,
            out_specs=[square_spec] * 5,
        ),
        out_shape=[
            jax.ShapeDtypeStruct(gram_l.shape, jnp.float32),
            jax.ShapeDtypeStruct(gram_l.shape, jnp.float32),
            jax.ShapeDtypeStruct(gram_l.shape, jnp.bfloat16),
            jax.ShapeDtypeStruct(gram_l.shape, jnp.bfloat16),
            jax.ShapeDtypeStruct(gram_l.shape, jnp.bfloat16),
        ],
        compiler_params=pltpu.CompilerParams(
            dimension_semantics=("arbitrary",), vmem_limit_bytes=VMEM_LIMIT
        ),
    )(block_row, block_col, due, hidden, grads, gram_l, gram_r, root_l, root_r)


def on_device(
    activations,
    cotangent,
    norm_gain,
    w_up,
    w_down,
    gram_left,
    gram_right,
    root_left,
    root_right,
    owner_slot,
    eighth,
    refresh_phase,
):
    low, f32 = jnp.bfloat16, jnp.float32
    section_no = lax.axis_index("section")
    dp_no = lax.axis_index("dp")
    mp_no = lax.axis_index("mp")
    dp_count = lax.axis_size("dp")
    mp_count = lax.axis_size("mp")
    micro_count, row_count, model_width = activations.shape
    rows = micro_count * row_count
    tokens = rows * dp_count
    up, down = w_up[0], w_down[0]
    width, shard_ff = up.shape
    is_first = section_no == 0
    gain = lax.dynamic_slice_in_dim(norm_gain[0], dp_no * width, width)

    block_cols = model_width // BLK
    block_rows = shard_ff // BLK
    group = block_rows * block_cols
    per_dev = gram_left.shape[1]
    pick = lambda table: lax.dynamic_slice_in_dim(
        lax.dynamic_index_in_dim(table, section_no, 0, keepdims=False), mp_no * block_rows, block_rows, 0
    ).reshape(-1)
    slots = (dp_no * mp_count + mp_no) * per_dev + jnp.arange(per_dev, dtype=jnp.int32)
    owned = pick(owner_slot)[None, :] == slots[:, None]
    block = jnp.sum(jnp.where(owned, jnp.arange(group, dtype=jnp.int32)[None, :], 0), axis=1)
    is_due = pick(eighth) == refresh_phase[0] % 8
    due = jnp.sum(jnp.where(owned & is_due[None, :], 1, 0), axis=1).astype(jnp.int32)

    mine = jnp.where(is_first, activations, cotangent).reshape(rows, dp_count, width)
    (start,) = swap_slots(0, [mine.transpose(1, 0, 2)], "dp")
    start_flat = start.reshape(tokens, width)

    def gained(flat):
        return (flat.astype(f32) * gain).astype(low)

    def row_squares(flat):
        values = flat.astype(f32)
        return jnp.sum(values * values, axis=-1).reshape(dp_count, rows)

    product = lax.cond(
        is_first,
        lambda: matmul(gained(start_flat), up).astype(low),
        lambda: matmul(start_flat, down).astype(low),
    )
    summed_a, squares = reduce_dp(
        1, product.reshape(dp_count, rows, shard_ff), row_squares(start_flat)
    )
    inverse_rms = lax.rsqrt(squares / model_width + norm_epsilon)
    hidden = jax.nn.silu(summed_a * inverse_rms[:, None]).astype(low)
    (hidden_a,) = gather_dp(3, [hidden])
    hidden_a = hidden_a.reshape(tokens, shard_ff)
    branch = matmul(hidden_a, down, 1, 1).astype(low)
    share = tokens // mp_count
    own_rows = lambda flat: lax.dynamic_slice_in_dim(flat, mp_no * share, share, 0)
    start_own = own_rows(start_flat)
    (relayed,) = relay(
        4,
        0,
        branch.reshape(mp_count, share, width),
        [start_own],
        lambda total, side, base: base.astype(f32) + total,
    )
    relayed = relayed.reshape(tokens, width)

    product = matmul(gained(relayed), up).astype(low)
    summed_b, squares = reduce_dp(
        6, product.reshape(dp_count, rows, shard_ff), row_squares(relayed)
    )
    inverse_rms = lax.rsqrt(squares / model_width + norm_epsilon)
    pre_act = summed_b * inverse_rms[:, None]
    hidden = jax.nn.silu(pre_act).astype(low)
    grad_pre = (summed_a * silu_slope(pre_act)).astype(low)
    row_dot = jnp.sum(summed_b * grad_pre.astype(f32), axis=-1)
    side = jnp.concatenate(
        [
            jnp.broadcast_to(inverse_rms[None], (8, rows)),
            jnp.broadcast_to(row_dot[None], (8, rows)),
        ]
    )
    grad_pre, side = gather_dp(8, [grad_pre, side])
    inverse_rms = own_rows(side[:, :, 0].reshape(tokens))[:, None]
    row_dot = side[:, :, 8].reshape(tokens, 1)
    dot_high = row_dot.astype(low)
    dot_low = (row_dot - lax.optimization_barrier(dot_high).astype(f32)).astype(low)
    dots = jnp.where(jnp.arange(128)[None, :] < 64, dot_high, dot_low)
    grad_normed = matmul(grad_pre.reshape(tokens, shard_ff), up, 1, 1).astype(low)
    spread = lambda column: jnp.broadcast_to(column, (share, 128))

    def input_gradient(total, side, base, values, rms, cubed, gain_row):
        row_dot = side[:, 0:1] + side[:, 64:65]
        return base.astype(f32) + (
            rms[:, 0:1] * (gain_row * total)
            - values.astype(f32) * (cubed[:, 0:1] * row_dot)
        )

    grad_relayed, hidden_b = relay(
        9,
        1,
        grad_normed.reshape(mp_count, share, width),
        [
            start_own,
            own_rows(relayed),
            spread(inverse_rms),
            spread(inverse_rms * inverse_rms * inverse_rms / model_width),
            gain[None],
        ],
        input_gradient,
        side=dots.reshape(mp_count, share, 128),
        aside=hidden,
    )
    grad_out = jnp.where(is_first, grad_relayed.reshape(tokens, width), start_flat)
    (grads,) = gather_dp(11, [grad_out])
    hidden_all = jnp.where(is_first, hidden_a, hidden_b.reshape(tokens, shard_ff))

    results = precondition(
        block // block_cols,
        block % block_cols,
        due,
        hidden_all,
        grads.reshape(dp_count, tokens, width),
        gram_left[0],
        gram_right[0],
        root_left[0],
        root_right[0],
    )
    return tuple(result[None] for result in results)


def solution(mesh):
    return jax.shard_map(
        on_device,
        mesh=mesh,
        in_specs=(
            P(None, "dp", None),
            P(None, "dp", None),
            P("section", None),
            P("section", "dp", "mp"),
            P("section", "dp", "mp"),
            P("section", ("dp", "mp"), None, None),
            P("section", ("dp", "mp"), None, None),
            P("section", ("dp", "mp"), None, None),
            P("section", ("dp", "mp"), None, None),
            P(),
            P(),
            P(),
        ),
        out_specs=(
            P("section", ("dp", "mp"), None, None),
            P("section", ("dp", "mp"), None, None),
            P("section", ("dp", "mp"), None, None),
            P("section", ("dp", "mp"), None, None),
            P("section", ("dp", "mp"), None, None),
        ),
        check_vma=False,
    )
```
